256 devices in a mesh: pipe: 2 (over y_hi), ctx: 16 (over y_lo, x, core), tp: 8 (over z).
Axes of the slice: x: 4, y: 4 (y_hi: 2, y_lo: 2; y = y_hi * 2 + y_lo), z: 8, core: 2. Of those that a mesh axis runs over, the one named last changes fastest.
Arguments:
- x_in: bfloat16 [2, 2048, 8192], P(None, 'ctx', 'tp'), may hold values from -6 to 6
- hidden_in: bfloat16 [2, 2048, 8192], P(None, ('ctx', 'tp')), may hold values from -6 to 6
- gate_z: bfloat16 [2, 2, 2048, 8192], P('pipe', None, 'ctx', 'tp'), may hold values from -6 to 6
- out_proj: bfloat16 [8192, 8192], P('tp', 'ctx'), may hold values from -0.0625 to 0.0625
- in_proj: bfloat16 [8192, 8192], P('tp', 'ctx'), may hold values from -0.0625 to 0.0625
- norm_gain: float32 [8192], replicated, may hold values from 0.1 to 1.9
- conv_weight: float32 [2, 4, 8192], P('pipe', None, 'tp'), may hold values from -3 to 3
- conv_bias: float32 [2, 8192], P('pipe', 'tp'), may hold values from -3 to 3
- x_proj: bfloat16 [2, 8192, 544], P('pipe', 'tp'), may hold values from -0.0625 to 0.0625
- dt_proj: bfloat16 [2, 512, 8192], P('pipe', None, 'tp'), may hold values from -0.25 to 0.25
- dt_bias: float32 [2, 8192], P('pipe', 'tp'), may hold values from -3 to -1
- decay_rate: float32 [2, 16, 8192], P('pipe', None, 'tp'), may hold values from 0.00048828125 to 1
- skip: float32 [2, 8192], P('pipe', 'tp'), may hold values from 0.1 to 1.9
Outputs:
- mixed: bfloat16 [2, 2, 2048, 8192], P('pipe', None, 'ctx', 'tp')
The draws below stay inside these ranges and needn't reach their ends.
All inputs are finite; a program needn't handle non-finite values.
Results may differ from the reference program's by a relative error of at most 0.017.
Values may be sent and summed in bfloat16 or wider, within the bound.
No kernel may reach another device: no remote copies, remote signals or barrier semaphores. Data moves between devices by JAX's collectives and lax.ppermute only.
A program may use at most 128 MiB of HBM per device.

```python
import math
import jax
import jax.numpy as jnp
from jax import lax

D = 8192
INNER = 8192
NSTATE = 16
RANK = 512
CONVW = 4
MICRO = 2
SECTIONS = 2
TOKENS = 2048


def steps_of(own_key, extent, pieces, least, top_value):
    loudness, own = 1.0, jax.random.fold_in(own_key, 6)
    for dim, blocks in pieces:
        heights = jnp.exp(jax.random.uniform(jax.random.fold_in(own, dim), (blocks,), jnp.float32, least / len(pieces), top_value / len(pieces)))
        loudness = loudness * jnp.repeat(heights, extent[dim] // blocks).reshape([-1 if axis == dim else 1 for axis in range(len(extent))])
    return loudness


def normal_values(own_key, shape, width, bound, split=(), held_as=jnp.bfloat16):
    gain = steps_of(own_key, shape, split, -0.22, 0.18) if split else 1.0
    values = jax.random.normal(own_key, shape, jnp.float32) * width * gain
    return jnp.minimum(jnp.maximum(values, -bound), bound).astype(held_as)


def setup_inputs(seed: int = 0) -> dict:
    key_list = jax.random.split(jax.random.key(seed), 14)
    x_in = normal_values(key_list[0], (MICRO, TOKENS, INNER), 1.0, 6.0, ((1, 16), (2, 8)))
    hidden_in = normal_values(key_list[1], (MICRO, TOKENS, D), 1.0, 6.0, ((1, 128),))
    gate_z = normal_values(key_list[2], (SECTIONS, MICRO, TOKENS, INNER), 1.0, 6.0, ((0, 2), (2, 16), (3, 8)))
    out_proj = normal_values(key_list[3], (INNER, D), INNER ** -0.5, 0.0625, ((0, 8), (1, 16)))
    in_proj = normal_values(key_list[4], (INNER, D), D ** -0.5, 0.0625, ((0, 8), (1, 16)))
    norm_gain = jnp.clip(1.0 + 0.18 * jax.random.normal(key_list[5], (D,), jnp.float32), 0.1, 1.9)
    conv_weight = normal_values(key_list[6], (SECTIONS, CONVW, INNER), CONVW ** -0.5, 3.0, ((0, 2), (2, 8)), jnp.float32)
    conv_bias = normal_values(key_list[7], (SECTIONS, INNER), 0.5, 3.0, ((0, 2), (1, 8)), jnp.float32)
    x_proj = normal_values(key_list[8], (SECTIONS, INNER, RANK + 2 * NSTATE), INNER ** -0.5, 0.0625, ((0, 2), (1, 8)))
    dt_proj = normal_values(key_list[9], (SECTIONS, RANK, INNER), RANK ** -0.5, 0.25, ((0, 2), (2, 8)))
    dt_bias = jnp.clip(-3.0 + 2.0 * jax.random.uniform(key_list[10], (SECTIONS, INNER), jnp.float32) ** steps_of(key_list[10], (SECTIONS, INNER), ((0, 2), (1, 8)), -0.2, 0.2), -3.0, -1.0)
    decay_rate = jnp.clip(jnp.exp(math.log(1.0) - 7.624619 * jax.random.uniform(key_list[11], (SECTIONS, NSTATE, INNER), jnp.float32) ** steps_of(key_list[11], (SECTIONS, NSTATE, INNER), ((0, 2), (2, 8)), -0.2, 0.2)), 0.00048828125, 1.0)
    skip = jnp.clip(1.0 + 0.18 * jax.random.normal(key_list[12], (SECTIONS, INNER), jnp.float32), 0.1, 1.9)
    return dict(x_in=x_in, hidden_in=hidden_in, gate_z=gate_z, out_proj=out_proj, in_proj=in_proj, norm_gain=norm_gain, conv_weight=conv_weight, conv_bias=conv_bias, x_proj=x_proj, dt_proj=dt_proj, dt_bias=dt_bias, decay_rate=decay_rate, skip=skip)


def run_section(inputs, gate, taps, bias, proj_weight, rate_weight, rate_bias, decay, skip_coef):
    count = inputs.shape[0]
    wide_in = inputs.astype(jnp.float32)
    padded = jnp.concatenate([jnp.zeros((CONVW - 1, INNER), jnp.float32), wide_in], axis=0)
    convolved = bias[None, :] + jnp.zeros((count, INNER), jnp.float32)
    for offset in range(CONVW):
        convolved = convolved + taps[offset][None, :] * padded[offset:offset + count]
    activated = jax.nn.silu(convolved).astype(jnp.bfloat16)
    projected = jnp.dot(activated, proj_weight, preferred_element_type=jnp.float32)
    rate_low = projected[:, :RANK]
    rate_normed = (rate_low * lax.rsqrt(lax.optimization_barrier(jnp.mean(rate_low * rate_low, axis=1, keepdims=True)) + 1e-06)).astype(jnp.bfloat16)
    step_size = jax.nn.softplus(jnp.dot(rate_normed, rate_weight, preferred_element_type=jnp.float32) + rate_bias[None, :])
    input_map = projected[:, RANK:RANK + NSTATE]
    output_map = projected[:, RANK + NSTATE:]
    active_wide = activated.astype(jnp.float32)

    def advance(state, row):
        step_row, act_row, in_row, out_row = row
        state = jnp.exp(-step_row[None, :] * decay) * state + in_row[:, None] * (step_row * act_row)[None, :]
        return (state, lax.optimization_barrier(jnp.sum(out_row[:, None] * state, axis=0)))
    start_state = jnp.zeros((NSTATE, INNER), jnp.float32)
    _, response = lax.scan(advance, start_state, (step_size, active_wide, input_map, output_map))
    response = response + skip_coef[None, :] * active_wide
    return (response * jax.nn.silu(gate.astype(jnp.float32))).astype(jnp.bfloat16)

def reference(x_in, hidden_in, gate_z, out_proj, in_proj, norm_gain, conv_weight, conv_bias, x_proj, dt_proj, dt_bias, decay_rate, skip):
    first_out = []
    second_out = []
    for batch in range(MICRO):
        mixed_first = run_section(x_in[batch], gate_z[0, batch], conv_weight[0], conv_bias[0], x_proj[0], dt_proj[0], dt_bias[0], decay_rate[0], skip[0])
        link = jnp.dot(mixed_first, out_proj, preferred_element_type=jnp.float32)
        carried = (hidden_in[batch].astype(jnp.float32) + link).astype(jnp.bfloat16)
        carried = lax.optimization_barrier(carried)
        wide = carried.astype(jnp.float32)
        normed = (wide * lax.rsqrt(lax.optimization_barrier(jnp.mean(wide * wide, axis=1, keepdims=True)) + 1e-05) * norm_gain[None, :]).astype(jnp.bfloat16)
        inputs = jnp.dot(normed, in_proj.T, preferred_element_type=jnp.float32).astype(jnp.bfloat16)
        mixed_second = run_section(inputs, gate_z[1, batch], conv_weight[1], conv_bias[1], x_proj[1], dt_proj[1], dt_bias[1], decay_rate[1], skip[1])
        first_out.append(mixed_first)
        second_out.append(mixed_second)
    return jnp.stack([jnp.stack(first_out, axis=0), jnp.stack(second_out, axis=0)], axis=0)
```

```python
import functools

import jax
import jax.numpy as jnp
from jax import lax
from jax.experimental import pallas as pl
from jax.experimental.pallas import tpu as pltpu
from jax.sharding import PartitionSpec as P

BF16 = jnp.bfloat16
F32 = jnp.float32
LOG2E = 1.4426950408889634
LANES = 128
SUBS = 8


def swap_pipe(block):
    return lax.ppermute(block, "pipe", [(0, 1), (1, 0)])


def swap_core(block):
    return lax.ppermute(block, "ctx", [(i, i ^ 1) for i in range(lax.axis_size("ctx"))])


def spread(block, axis):
    copies = jnp.broadcast_to(block[None], (lax.axis_size(axis), *block.shape))
    return lax.all_to_all(copies, axis, 0, 0)


def halo(block, rows):
    size = lax.axis_size("ctx")
    return lax.ppermute(block[block.shape[0] - rows :], "ctx", [(i, i + 1) for i in range(size - 1)])


def convolve(inputs, rim, conv_weight, conv_bias):
    count = inputs.shape[0]
    padded = jnp.concatenate([rim, inputs], axis=0).astype(F32)
    total = conv_bias
    for offset in range(conv_weight.shape[0]):
        total = total + conv_weight[offset][None, :] * padded[offset : offset + count]
    return jax.nn.silu(total).astype(BF16)


def advance(states, decay_ref, step, drive, maps_ref, token):
    out = []
    for n, state in enumerate(states):
        keep = jnp.exp2(step * decay_ref[n * SUBS : (n + 1) * SUBS, :])
        out.append(keep * state + maps_ref[token, n] * drive)
    return out


def fold_kernel(maps_ref, rate_ref, dtw_ref, dtb_ref, act_ref, decay_ref, step_ref, drive_ref, end_ref):
    count, width = act_ref.shape
    nstate = decay_ref.shape[0] // SUBS
    wide = 2 * LANES
    for j in range(width // wide):
        cols = slice(j * wide, (j + 1) * wide)
        raw = jnp.dot(rate_ref[...], dtw_ref[:, cols], preferred_element_type=F32) + dtb_ref[:, cols]
        step = jnp.maximum(raw, 0.0) + jnp.log1p(jnp.exp(-jnp.abs(raw)))
        drive = step * act_ref[:, cols].astype(F32)
        for half in range(2):
            part = slice(half * LANES, (half + 1) * LANES)
            step_ref[pl.ds(2 * j + half, count, stride=SUBS), :] = step[:, part]
            drive_ref[pl.ds(2 * j + half, count, stride=SUBS), :] = drive[:, part]

    def one(token, carry):
        states, total = carry
        rows = pl.ds(pl.multiple_of(token * SUBS, SUBS), SUBS)
        step = step_ref[rows, :]
        states = advance(states, decay_ref, step, drive_ref[rows, :], maps_ref, token)
        return (states, total + step)

    zero = jnp.zeros((SUBS, LANES), F32)
    states, total = lax.fori_loop(0, count, one, ([zero] * nstate, zero), unroll=4)
    for n in range(nstate):
        end_ref[n * SUBS : (n + 1) * SUBS, :] = states[n]
    end_ref[nstate * SUBS : (nstate + 1) * SUBS, :] = total


def fold_states(maps, rate, dtw, dtb, act, decay):
    count, width = act.shape
    rows = count * width // LANES
    ends = decay.shape[0] + SUBS
    vmem = pl.BlockSpec(memory_space=pltpu.VMEM)
    return pl.pallas_call(
        fold_kernel,
        out_shape=(
            jax.ShapeDtypeStruct((rows, LANES), F32),
            jax.ShapeDtypeStruct((rows, LANES), F32),
            jax.ShapeDtypeStruct((ends, LANES), F32),
        ),
        in_specs=[pl.BlockSpec(memory_space=pltpu.SMEM)] + [vmem] * 5,
        out_specs=(vmem, vmem, vmem),
        name="fold_states",
    )(maps, rate, dtw, dtb, act, decay)


def respond_kernel(
    place_ref, maps_ref, carry_ref, decay_ref, step_ref, drive_ref, act_ref, skip_ref, gate_ref, out_ref, resp_ref
):
    count, width = act_ref.shape
    nstate = decay_ref.shape[0] // SUBS

    def link(block, states):
        got = carry_ref[block].astype(F32)
        total = got[nstate * SUBS : (nstate + 1) * SUBS] + got[(nstate + 1) * SUBS :]
        out = []
        for n, state in enumerate(states):
            keep = jnp.exp2(total * decay_ref[n * SUBS : (n + 1) * SUBS, :])
            out.append(keep * state + got[n * SUBS : (n + 1) * SUBS])
        return out

    zero = jnp.zeros((SUBS, LANES), F32)
    states = lax.fori_loop(0, place_ref[0], link, [zero] * nstate)

    def one(token, states):
        rows = pl.ds(pl.multiple_of(token * SUBS, SUBS), SUBS)
        states = advance(states, decay_ref, step_ref[rows, :], drive_ref[rows, :], maps_ref, token)
        sums = [maps_ref[token, nstate + n] * states[n] for n in range(nstate)]
        while len(sums) > 1:
            sums = [a + b for a, b in zip(sums[0::2], sums[1::2])]
        resp_ref[rows, :] = sums[0]
        return states

    lax.fori_loop(0, count, one, states, unroll=4)
    for j in range(width // LANES):
        cols = slice(j * LANES, (j + 1) * LANES)
        response = resp_ref[pl.ds(j, count, stride=SUBS), :] + skip_ref[:, cols] * act_ref[:, cols].astype(F32)
        gate = gate_ref[:, cols].astype(F32)
        out_ref[:, cols] = (response * (gate / (1.0 + jnp.exp(-gate)))).astype(BF16)


def respond(place, maps, carry, decay, step, drive, act, skip, gate):
    vmem = pl.BlockSpec(memory_space=pltpu.VMEM)
    smem = pl.BlockSpec(memory_space=pltpu.SMEM)
    return pl.pallas_call(
        respond_kernel,
        out_shape=jax.ShapeDtypeStruct(act.shape, BF16),
        in_specs=[smem, smem] + [vmem] * 7,
        out_specs=vmem,
        scratch_shapes=[pltpu.VMEM(step.shape, F32)],
        name="respond",
    )(place, maps, carry, decay, step, drive, act, skip, gate)


def mixer(inputs, rim, gate, weights):
    conv_weight, conv_bias, x_proj, dt_proj, dt_bias, decay, skip = weights
    count, width = inputs.shape
    rank = dt_proj.shape[0]
    parts = lax.axis_size("tp")
    act = convolve(inputs, rim, conv_weight, conv_bias)
    partial = jnp.dot(act, x_proj, preferred_element_type=F32).astype(BF16)
    pieces = lax.all_to_all(partial.reshape(parts, count // parts, -1), "tp", 0, 0)
    share = jnp.sum(pieces.astype(F32), axis=0)
    low = share[:, :rank]
    low = low * lax.rsqrt(jnp.mean(low * low, axis=1, keepdims=True) + 1e-06)
    share = jnp.concatenate([low, share[:, rank:]], axis=1).astype(BF16)
    full = spread(share, "tp").reshape(count, -1)
    rate = full[:, :rank]
    maps = full[:, rank:].astype(F32)
    decay2 = (decay * (-LOG2E)).reshape(-1, LANES)
    step, drive, end = fold_states(maps, rate, dt_proj, dt_bias, act, decay2)
    nrows = decay2.shape[0]
    total = end[nrows:]
    high = total.astype(BF16)
    low_part = (total - high.astype(F32)).astype(BF16)
    carry = spread(jnp.concatenate([end[:nrows].astype(BF16), high, low_part], axis=0), "ctx")
    place = lax.axis_index("ctx").astype(jnp.int32).reshape(1)
    return respond(place, maps, carry, decay2, step, drive, act, skip, gate), end


def after(value, *others):
    return lax.optimization_barrier((value, *others))[0]


def swap_row(block):
    size = lax.axis_size("ctx")
    return lax.ppermute(block, "ctx", [(i, (i + size // 2) % size) for i in range(size)])


def swap_halves(block):
    half = block.shape[0] // 2
    core = lax.axis_index("ctx") % 2
    mine = swap_pipe(lax.dynamic_slice_in_dim(block, core * half, half, 0))
    theirs = swap_core(mine)
    return jnp.where(core == 0, jnp.concatenate([mine, theirs]), jnp.concatenate([theirs, mine]))


def gather_row(weight):
    size = lax.axis_size("ctx")
    groups = [list(range(size // 2)), list(range(size // 2, size))]
    return lax.all_gather(weight, "ctx", axis=0, axis_index_groups=groups)


def around(block, distance):
    size = lax.axis_size("tp")
    return lax.ppermute(block, "tp", [(i, (i + distance) % size) for i in range(size)])


def ring_reduce(piece):
    size = lax.axis_size("tp")
    me = lax.axis_index("tp")
    at = lambda d: piece((me + d + size) % size)
    far = at(size // 2)
    half = far.shape[0] // 2
    right = around(far[:half].astype(BF16), 1)
    left = around(far[half:].astype(BF16), -1)
    for d in range(size // 2 - 1, 0, -1):
        ahead, behind = at(d), at(-d)
        if right.shape[0] == half:
            ahead = jnp.concatenate([ahead[:half] + right.astype(F32), ahead[half:]])
            behind = jnp.concatenate([behind[:half], behind[half:] + left.astype(F32)])
        else:
            ahead, behind = ahead + right.astype(F32), behind + left.astype(F32)
        right, left = around(ahead.astype(BF16), 1), around(behind.astype(BF16), -1)
    return at(0) + right.astype(F32) + left.astype(F32)


def ring_gather(block):
    size = lax.axis_size("tp")
    me = lax.axis_index("tp")
    half = block.shape[0] // 2
    yield me, block
    right = left = block
    for d in range(1, size // 2):
        right, left = around(right, 1), around(left, -1)
        yield (me - d + size) % size, right
        yield (me + d) % size, left
    far = jnp.concatenate([around(right[:half], 1), around(left[half:], -1)])
    yield (me + size // 2) % size, far


def shards(
    x_in,
    hidden_in,
    gate_z,
    out_proj,
    in_proj,
    norm_gain,
    conv_weight,
    conv_bias,
    x_proj,
    dt_proj,
    dt_bias,
    decay_rate,
    skip,
):
    pipe = lax.axis_index("pipe")
    parts = lax.axis_size("tp")
    row = lax.axis_index("ctx") // (lax.axis_size("ctx") // 2)
    first = pipe == 0
    taps = conv_weight.shape[1]
    nstate = decay_rate.shape[1]
    pick = lambda array, index: lax.dynamic_index_in_dim(array, index, 0, False)

    out_row = gather_row(out_proj)
    inputs = pick(x_in, pipe)
    rim = halo(inputs, taps - 1)
    small = jnp.concatenate([conv_weight[0], conv_bias, dt_bias, skip, decay_rate[0]], axis=0)
    small_other = swap_pipe(small)
    x_proj_other = swap_halves(x_proj[0])
    dt_proj_other = swap_halves(after(dt_proj[0], x_proj_other))
    gate_own = pick(gate_z[0], pipe)
    gate_other = swap_pipe(after(pick(gate_z[0], 1 - pipe), dt_proj_other))

    def section(flag):
        pack = jnp.where(flag, small, small_other)
        return (
            (
                pack[:taps],
                pack[taps : taps + 1],
                jnp.where(flag, x_proj[0], x_proj_other),
                jnp.where(flag, dt_proj[0], dt_proj_other),
                pack[taps + 1 : taps + 2],
                pack[taps + 3 : taps + 3 + nstate],
                pack[taps + 2 : taps + 3],
            ),
            jnp.where(flag, gate_own, gate_other),
        )

    weights, gate = section(first)
    mixed_first, mark = mixer(inputs, rim, gate, weights)
    in_row = gather_row(after(in_proj, mark))

    count, width = mixed_first.shape
    chunks, _, cols = out_row.shape
    hidden = pick(hidden_in, pipe).reshape(-1, 2, chunks, cols).transpose(1, 2, 0, 3)
    hidden = jnp.stack([pick(hidden, row), swap_row(pick(hidden, 1 - row))], axis=1)
    share = hidden.shape[2]
    me = lax.axis_index("tp")
    padded = lax.dynamic_update_slice(
        jnp.zeros((chunks, 2, count, cols), BF16), hidden, (0, 0, me * share, 0)
    ).reshape(chunks, 2 * count, cols)
    both = jnp.concatenate([mixed_first, swap_row(mixed_first)])

    def piece(place):
        link = jnp.dot(both, pick(out_row, place), preferred_element_type=F32)
        return link + pick(padded, place).astype(F32)

    carried = ring_reduce(piece).astype(BF16)
    gain = pick(norm_gain.reshape(2, chunks, cols), row)
    total = jnp.zeros((2 * count, width), F32)
    squares = jnp.zeros((2 * count, 1), F32)
    for place, block in ring_gather(carried):
        wide = block.astype(F32)
        squares = squares + jnp.sum(wide * wide, axis=1, keepdims=True)
        scaled = (wide * pick(gain, place)[None, :]).astype(BF16)
        total = total + lax.dot_general(
            scaled, pick(in_row, place), (((1,), (1,)), ((), ())), preferred_element_type=F32
        )
    squares = squares[:count] + swap_row(squares[count:])
    total = total[:count] + swap_row(total[count:].astype(BF16)).astype(F32)
    inputs = (total * lax.rsqrt(squares / (2 * chunks * cols) + 1e-05)).astype(BF16)

    weights, gate = section(jnp.logical_not(first))
    mixed_second, _ = mixer(inputs, halo(inputs, taps - 1), gate, weights)
    keep = jnp.where(first, mixed_first, mixed_second)
    other = swap_pipe(jnp.where(first, mixed_second, mixed_first))
    return jnp.where(first, jnp.stack([keep, other]), jnp.stack([other, keep]))[None]


def solution(mesh):
    in_specs = (
        P(None, "ctx", "tp"),
        P(None, ("ctx", "tp"), None),
        P("pipe", None, "ctx", "tp"),
        P("tp", "ctx"),
        P("tp", "ctx"),
        P(),
        P("pipe", None, "tp"),
        P("pipe", "tp"),
        P("pipe", "tp", None),
        P("pipe", None, "tp"),
        P("pipe", "tp"),
        P("pipe", None, "tp"),
        P("pipe", "tp"),
    )
    out_specs = P("pipe", None, "ctx", "tp")
    return jax.shard_map(shards, mesh=mesh, in_specs=in_specs, out_specs=out_specs, check_vma=False)
```

```python
import jax
import jax.numpy as jnp
from jax import lax
from jax.experimental import pallas as pl
from jax.experimental.pallas import tpu as pltpu
from jax.sharding import PartitionSpec as P

BF16 = jnp.bfloat16
F32 = jnp.float32
LOG2E = 1.4426950408889634
LANES = 128
SUBS = 8


def swap_pipe(block):
    return lax.ppermute(block, "pipe", [(0, 1), (1, 0)])


def swap_core(block):
    return lax.ppermute(block, "ctx", [(i, i ^ 1) for i in range(lax.axis_size("ctx"))])


def spread(block, axis):
    copies = jnp.broadcast_to(block[None], (lax.axis_size(axis), *block.shape))
    return lax.all_to_all(copies, axis, 0, 0)


def halo(block, rows):
    size = lax.axis_size("ctx")
    return lax.ppermute(block[block.shape[0] - rows :], "ctx", [(i, i + 1) for i in range(size - 1)])


def convolve(inputs, rim, conv_weight, conv_bias):
    count = inputs.shape[0]
    padded = jnp.concatenate([rim, inputs], axis=0).astype(F32)
    total = conv_bias
    for offset in range(conv_weight.shape[0]):
        total = total + conv_weight[offset][None, :] * padded[offset : offset + count]
    return jax.nn.silu(total).astype(BF16)


def advance(states, decay_ref, step, drive, maps_ref, token):
    out = []
    for n, state in enumerate(states):
        keep = jnp.exp2(step * decay_ref[n * SUBS : (n + 1) * SUBS, :])
        out.append(keep * state + maps_ref[token, n] * drive)
    return out


def fold_kernel(
    flags_ref, maps_ref, rate_ref, own_ref, mine_ref, theirs_ref, dtb_ref, act_ref, decay_ref,
    step_ref, drive_ref, end_ref, dtw_ref, sem,
):
    rows = mine_ref.shape[0]
    core = flags_ref[1]

    def run(*copies):
        for copy in copies:
            copy.start()
        for copy in copies:
            copy.wait()

    @pl.when(flags_ref[0] == 1)
    def _():
        run(pltpu.make_async_copy(own_ref, dtw_ref, sem.at[0]))

    @pl.when(flags_ref[0] == 0)
    def _():
        mine = dtw_ref.at[pl.ds(pl.multiple_of(core * rows, rows), rows)]
        theirs = dtw_ref.at[pl.ds(pl.multiple_of((1 - core) * rows, rows), rows)]
        run(pltpu.make_async_copy(mine_ref, mine, sem.at[0]), pltpu.make_async_copy(theirs_ref, theirs, sem.at[1]))

    count, width = act_ref.shape
    nstate = decay_ref.shape[0] // SUBS
    wide = 2 * LANES

    for j in range(width // wide):
        cols = slice(j * wide, (j + 1) * wide)
        raw = jnp.dot(rate_ref[...], dtw_ref[:, cols], preferred_element_type=F32) + dtb_ref[:, cols]
        step = jnp.maximum(raw, 0.0) + jnp.log1p(jnp.exp(-jnp.abs(raw)))
        drive = step * act_ref[:, cols].astype(F32)
        for half in range(2):
            part = slice(half * LANES, (half + 1) * LANES)
            step_ref[pl.ds(2 * j + half, count, stride=SUBS), :] = step[:, part]
            drive_ref[pl.ds(2 * j + half, count, stride=SUBS), :] = drive[:, part]

    def one(token, carry):
        states, total = carry
        rows = pl.ds(pl.multiple_of(token * SUBS, SUBS), SUBS)
        step = step_ref[rows, :]
        states = advance(states, decay_ref, step, drive_ref[rows, :], maps_ref, token)
        return (states, total + step)

    zero = jnp.zeros((SUBS, LANES), F32)
    states, total = lax.fori_loop(0, count, one, ([zero] * nstate, zero), unroll=4)
    high = total.astype(BF16).astype(F32)
    pairs = [*zip(states[0::2], states[1::2]), (high, total - high)]
    for n, pair in enumerate(pairs):
        tile = jnp.concatenate(pair, axis=0).astype(BF16)
        for copy in range(end_ref.shape[0]):
            end_ref[copy, n * 2 * SUBS : (n + 1) * 2 * SUBS, :] = tile


def fold_states(flags, maps, rate, dtw, dtb, act, decay, copies):
    count, width = act.shape
    rows = count * width // LANES
    ends = decay.shape[0] + 2 * SUBS
    vmem = pl.BlockSpec(memory_space=pltpu.VMEM)
    smem = pl.BlockSpec(memory_space=pltpu.SMEM)
    left = pl.BlockSpec(memory_space=pl.ANY)
    return pl.pallas_call(
        fold_kernel,
        out_shape=(
            jax.ShapeDtypeStruct((rows, LANES), F32),
            jax.ShapeDtypeStruct((rows, LANES), F32),
            jax.ShapeDtypeStruct((copies, ends, LANES), BF16),
        ),
        in_specs=[smem, smem, vmem, left, left, left, vmem, vmem, vmem],
        out_specs=(vmem, vmem, vmem),
        scratch_shapes=[pltpu.VMEM(dtw[0].shape, BF16), pltpu.SemaphoreType.DMA((2,))],
        name="fold_states",
    )(flags, maps, rate, *dtw, dtb, act, decay)


def respond_kernel(
    place_ref, maps_ref, carry_ref, decay_ref, step_ref, drive_ref, act_ref, skip_ref, gate_ref, out_ref, resp_ref
):
    count, width = act_ref.shape
    nstate = decay_ref.shape[0] // SUBS

    def link(block, states):
        got = carry_ref[block].astype(F32)
        total = got[nstate * SUBS : (nstate + 1) * SUBS] + got[(nstate + 1) * SUBS :]
        out = []
        for n, state in enumerate(states):
            keep = jnp.exp2(total * decay_ref[n * SUBS : (n + 1) * SUBS, :])
            out.append(keep * state + got[n * SUBS : (n + 1) * SUBS])
        return out

    zero = jnp.zeros((SUBS, LANES), F32)
    states = lax.fori_loop(0, place_ref[0], link, [zero] * nstate)

    def one(token, states):
        rows = pl.ds(pl.multiple_of(token * SUBS, SUBS), SUBS)
        states = advance(states, decay_ref, step_ref[rows, :], drive_ref[rows, :], maps_ref, token)
        sums = [maps_ref[token, nstate + n] * states[n] for n in range(nstate)]
        while len(sums) > 1:
            sums = [a + b for a, b in zip(sums[0::2], sums[1::2])]
        resp_ref[rows, :] = sums[0]
        return states

    lax.fori_loop(0, count, one, states, unroll=4)

    @pl.loop(0, width // LANES)
    def _(j):
        cols = pl.ds(pl.multiple_of(j * LANES, LANES), LANES)
        response = resp_ref[pl.ds(j, count, stride=SUBS), :] + skip_ref[:, cols] * act_ref[:, cols].astype(F32)
        gate = gate_ref[:, cols].astype(F32)
        out_ref[:, cols] = (response * (gate / (1.0 + jnp.exp(-gate)))).astype(BF16)


def respond(place, maps, carry, decay, step, drive, act, skip, gate):
    vmem = pl.BlockSpec(memory_space=pltpu.VMEM)
    smem = pl.BlockSpec(memory_space=pltpu.SMEM)
    return pl.pallas_call(
        respond_kernel,
        out_shape=jax.ShapeDtypeStruct(act.shape, BF16),
        in_specs=[smem, smem] + [vmem] * 7,
        out_specs=vmem,
        scratch_shapes=[pltpu.VMEM(step.shape, F32)],
        name="respond",
    )(place, maps, carry, decay, step, drive, act, skip, gate)


def shared_rates(partial, rank):
    parts = lax.axis_size("tp")
    batch, count, cols = partial.shape
    pieces = partial.reshape(batch, parts, count // parts, cols).transpose(1, 0, 2, 3)
    share = jnp.sum(lax.all_to_all(pieces, "tp", 0, 0).astype(F32), axis=0)
    low = share[:, :, :rank]
    low = low * lax.rsqrt(jnp.mean(low * low, axis=2, keepdims=True) + 1e-06)
    return jnp.concatenate([low, share[:, :, rank:]], axis=2).astype(BF16)


def mixer(act, full, gate, weights):
    flags, dt_proj, dt_bias, decay, skip = weights
    rank = dt_proj[0].shape[0]
    full = full.reshape(act.shape[0], -1)
    rate = full[:, :rank]
    maps = full[:, rank:].astype(F32)
    decay2 = (decay * (-LOG2E)).reshape(-1, LANES)
    step, drive, ends = fold_states(flags, maps, rate, dt_proj, dt_bias, act, decay2, lax.axis_size("ctx"))
    carry = lax.all_to_all(ends, "ctx", 0, 0)
    place = lax.axis_index("ctx").astype(jnp.int32).reshape(1)
    return respond(place, maps, carry, decay2, step, drive, act, skip, gate)


def swap_row(block):
    size = lax.axis_size("ctx")
    return lax.ppermute(block, "ctx", [(i, (i + size // 2) % size) for i in range(size)])


def swap_halves(block):
    half = block.shape[0] // 2
    core = lax.axis_index("ctx") % 2
    mine = swap_pipe(lax.dynamic_slice_in_dim(block, core * half, half, 0))
    return mine, swap_core(mine)


def gather_row(weight):
    size = lax.axis_size("ctx")
    groups = [list(range(size // 2)), list(range(size // 2, size))]
    return lax.all_gather(weight, "ctx", axis=0, axis_index_groups=groups)


def around(block, distance):
    size = lax.axis_size("tp")
    return lax.ppermute(block, "tp", [(i, (i + distance) % size) for i in range(size)])


def held(*values):
    return lax.optimization_barrier(values)


def ring_reduce(lead, piece):
    far = lax.axis_size("tp") // 2
    right = around(lead(0).astype(BF16), 1)
    left = around(lead(1).astype(BF16), -1)
    half = right.shape[0]
    for d in range(far - 1, 0, -1):
        ahead, behind = held(piece(d))[0], held(piece(-d))[0]
        if d == far - 1:
            ahead = jnp.concatenate([ahead[:half] + right.astype(F32), ahead[half:]])
            behind = jnp.concatenate([behind[:half], behind[half:] + left.astype(F32)])
        else:
            ahead, behind = ahead + right.astype(F32), behind + left.astype(F32)
        right = around(ahead.astype(BF16), 1)
        left = around(behind.astype(BF16), -1)
    return held(piece(0))[0] + right.astype(F32) + left.astype(F32)


def ring_gather(block, take):
    size = lax.axis_size("tp")
    me = lax.axis_index("tp")
    far = size // 2
    half = block.shape[0] // 2
    right = left = block
    for d in range(1, far):
        before = right, left
        right, left = around(right, 1), around(left, -1)
        take((me - d + 1 + size) % size, before[0], f"t{d}R")
        if d > 1:
            take((me + d - 1) % size, before[1], f"t{d}L")
    last = around(right[:half], 1), around(left[half:], -1)
    take((me - far + 1 + size) % size, right, f"t{far}R")
    take((me + far - 1) % size, left, f"t{far}L")
    take((me + far) % size, jnp.concatenate(last), "t")


def shards(
    x_in,
    hidden_in,
    gate_z,
    out_proj,
    in_proj,
    norm_gain,
    conv_weight,
    conv_bias,
    x_proj,
    dt_proj,
    dt_bias,
    decay_rate,
    skip,
):
    pipe = lax.axis_index("pipe")
    row = lax.axis_index("ctx") // (lax.axis_size("ctx") // 2)
    first = pipe == 0
    taps = conv_weight.shape[1]
    nstate = decay_rate.shape[1]
    rank = dt_proj.shape[1]
    pick = lambda array, index: lax.dynamic_index_in_dim(array, index, 0, False)

    out_row = gather_row(out_proj)
    small = jnp.concatenate([conv_weight[0], conv_bias, dt_bias, skip, decay_rate[0]], axis=0)
    small_other = swap_pipe(small)
    size = lax.axis_size("ctx")
    rims = lax.ppermute(x_in[:, x_in.shape[1] - (taps - 1) :], "ctx", [(i, i + 1) for i in range(size - 1)])
    dt_proj_other = swap_halves(dt_proj[0])
    gate_own = pick(gate_z[0], pipe)
    gate_other = swap_pipe(pick(gate_z[0], 1 - pipe))
    x_proj_other = swap_pipe(x_proj[0])

    def section(flag):
        pack = jnp.where(flag, small, small_other)
        return (
            (pack[:taps], pack[taps : taps + 1]),
            (
                jnp.stack([flag.astype(jnp.int32), lax.axis_index("ctx") % 2]),
                (dt_proj[0], *dt_proj_other),
                pack[taps + 1 : taps + 2],
                pack[taps + 3 : taps + 3 + nstate],
                pack[taps + 2 : taps + 3],
            ),
            jnp.where(flag, gate_own, gate_other),
        )

    conv, weights, gate = section(first)
    acts = jnp.stack([convolve(x_in[m], rims[m], *conv) for m in range(x_in.shape[0])])
    partial = jnp.einsum("mtk,kr->mtr", acts, x_proj[0], preferred_element_type=F32).astype(BF16)
    shares = shared_rates(partial, rank)
    tp = lax.axis_size("tp")
    copies = jnp.broadcast_to(shares[:, None], (2, tp, *shares.shape[1:])).reshape(2 * tp, *shares.shape[1:])
    full = lax.all_to_all(copies, ("pipe", "tp"), 0, 0)[:tp]
    mixed_first = mixer(pick(acts, pipe), full, gate, weights)
    in_row = gather_row(in_proj)

    count, width = mixed_first.shape
    chunks, _, cols = out_row.shape
    hidden = pick(hidden_in, pipe).reshape(-1, 2, chunks, cols).transpose(1, 2, 0, 3)
    hidden = [pick(hidden, row), swap_row(pick(hidden, 1 - row))]
    tall = hidden[0].shape[1]
    me = lax.axis_index("tp")
    zero = jnp.zeros((chunks, count, cols), BF16)
    zero = jnp.zeros((chunks, count, cols), BF16)
    padded = jnp.concatenate([lax.dynamic_update_slice(zero, rows, (0, me * tall, 0)) for rows in hidden], axis=1)
    swapped = swap_row(mixed_first)
    both = jnp.concatenate([mixed_first, swapped])
    other_first = swap_pipe(mixed_first)

    far = tp // 2
    early = (far, far - 1, 1 - far)
    ahead = dict(zip(early, held(*(pick(out_row, (me + d + tp) % tp) for d in early))))

    def lead(s):
        link = jnp.dot((mixed_first, swapped)[s], ahead[far], preferred_element_type=F32)
        return link + pick(padded, (me + far) % tp)[s * count : (s + 1) * count].astype(F32)

    def piece(d):
        place = (me + d + tp) % tp
        weight = ahead[d] if d in ahead else pick(out_row, place)
        link = jnp.dot(both, weight, preferred_element_type=F32)
        return link + pick(padded, place).astype(F32)

    carried = ring_reduce(lead, piece).astype(BF16)
    gain = pick(norm_gain.reshape(2, chunks, cols), row)
    total = [jnp.zeros((2 * count, width), F32)]
    squares = [jnp.zeros((2 * count, LANES), F32)]
    ones = jnp.ones((cols, LANES), BF16)

    def take(place, block, name):
        wide = block.astype(F32)
        squares[0] = squares[0] + jnp.dot((wide * wide).astype(BF16), ones, preferred_element_type=F32)
        scaled = (wide * pick(gain, place)[None, :]).astype(BF16)
        weight = pick(in_row, place)
        parts = [slice(count, None), slice(0, count)] if name == "t" else [slice(None)]
        sums = []
        for rows in parts:
            sums.append(
                total[0][rows]
                + lax.dot_general(
                    scaled[rows], weight, (((1,), (1,)), ((), ())), preferred_element_type=F32
                )
            )
        total[:] = sums

    ring_gather(carried, take)
    squares = squares[0]
    sent = jnp.concatenate([total[0].astype(BF16), squares[count:].astype(BF16)], axis=1)
    got = swap_row(sent).astype(F32)
    scale = lax.rsqrt((squares[:count] + got[:, width:]) / (2 * chunks * cols) + 1e-05)
    inputs = ((total[1] + got[:, :width]) * jnp.concatenate([scale] * (width // LANES), axis=1)).astype(BF16)

    conv, weights, gate = section(jnp.logical_not(first))
    act = convolve(inputs, halo(inputs, taps - 1), *conv)
    own = jnp.dot(act, x_proj[0], preferred_element_type=F32)
    other = jnp.dot(act, x_proj_other, preferred_element_type=F32)
    partial = jnp.where(first, other, own).astype(BF16)
    share = shared_rates(partial[None], rank)[0]
    mixed_second = mixer(act, spread(share, "tp"), gate, weights)
    late = swap_pipe(mixed_second)
    return jnp.where(first, jnp.stack([mixed_first, other_first]), jnp.stack([late, mixed_second]))[None]


def solution(mesh):
    in_specs = (
        P(None, "ctx", "tp"),
        P(None, ("ctx", "tp"), None),
        P("pipe", None, "ctx", "tp"),
        P("tp", "ctx"),
        P("tp", "ctx"),
        P(),
        P("pipe", None, "tp"),
        P("pipe", "tp"),
        P("pipe", "tp", None),
        P("pipe", None, "tp"),
        P("pipe", "tp"),
        P("pipe", None, "tp"),
        P("pipe", "tp"),
    )
    out_specs = P("pipe", None, "ctx", "tp")

    return jax.shard_map(shards, mesh=mesh, in_specs=in_specs, out_specs=out_specs, check_vma=False)
```
